256 devices in a mesh: ckpt: 4 (over z_lo), tok: 64 (over y, z_hi, x, core).
Axes of the slice: x: 4, y: 4, z: 8 (z_hi: 2, z_lo: 4; z = z_hi * 4 + z_lo), core: 2. Of those that a mesh axis runs over, the one named last changes fastest.
Arguments:
- features: bfloat16 [4, 8192, 1792], P('ckpt', 'tok'), may hold values from -22 to 22
- pairing: int32 [4, 64, 128], P('ckpt', 'tok'), may hold values from 0 to 127, each once within a row
- rotation: bfloat16 [4, 1792, 1792], P('ckpt', 'tok'), may hold values from -1 to 2
Outputs:
- consensus: bfloat16 [8192, 1792], P('tok')
- rotation_next: bfloat16 [4, 1792, 1792], P('ckpt', 'tok')
The draws below stay inside these ranges and needn't reach their ends.
Inputs may be any that keep to these rules, and one draw needn't show every extreme that they name: Each row of a shard of 128 rows appears once in that shard's pairing.
All inputs are finite; a program needn't handle non-finite values.
Results may differ from the reference program's by a relative error of at most 0.011.
Values may be sent and summed in bfloat16 or wider, within the bound.
A program may use at most 64 MiB of HBM per device.

```python
import math
import jax
import jax.numpy as jnp
from jax import lax

W = 1792
TOK_DEV = 128
CKPTS = 4
TOKENS = 8192
N_TOK = 64


def draw_features(key, part):
    base_key, column_key = jax.random.split(key, 2)
    columns = jnp.exp(0.5 * jax.random.uniform(column_key, (CKPTS, 1, W), jnp.float32, 0.0, math.log(10.0)))
    values = jnp.clip(jax.random.normal(base_key, (CKPTS, TOKENS, W), jnp.float32), -4.5, 4.5)
    return (values * columns).astype(jnp.bfloat16)


def draw_rotation(key, part):
    noise_key, diagonal_key = jax.random.split(key, 2)
    row_index = lax.broadcasted_iota(jnp.int32, (1, W, 1), 1)
    col_index = lax.broadcasted_iota(jnp.int32, (1, 1, W), 2)
    identity = (row_index == col_index).astype(jnp.float32)
    diagonal = jax.random.uniform(diagonal_key, (CKPTS, 1, W), jnp.float32, 0.75, 1.25)
    noise = jnp.clip(jax.random.normal(noise_key, (CKPTS, W, W), jnp.float32), -4.5, 4.5)
    return (identity * diagonal + 0.5 / math.sqrt(W) * noise).astype(jnp.bfloat16)


def setup_inputs(seed: int = 0) -> dict:
    key_of = jax.random.split(jax.random.key(seed), 4)
    features = draw_features(jax.random.fold_in(key_of[3], 71), 0)
    pairing = jax.vmap(lambda own: jax.random.permutation(own, TOK_DEV))(jax.random.split(key_of[1], CKPTS * N_TOK)).reshape((CKPTS, N_TOK, TOK_DEV)).astype(jnp.int32)
    rotation = draw_rotation(jax.random.fold_in(key_of[3], 71), 0)
    return dict(features=features, pairing=pairing, rotation=rotation)


def apply_once(vector, start_mat):
    inner = jnp.dot(vector.astype(jnp.bfloat16), start_mat.T, preferred_element_type=jnp.float32).astype(jnp.bfloat16)
    return jnp.dot(inner, start_mat, preferred_element_type=jnp.float32)

def reference(features, pairing, rotation):
    offsets = (jnp.arange(N_TOK, dtype=jnp.int32) * TOK_DEV)[:, None]
    aligned_list = []
    running = jnp.zeros((TOKENS, W), jnp.float32)
    for member in range(CKPTS):
        index = (pairing[member].astype(jnp.int32) + offsets).reshape(-1).astype(jnp.int32)
        aligned = jnp.take(features[member], index, axis=0)
        aligned_list.append(aligned)
        rotated = jnp.dot(aligned, rotation[member], preferred_element_type=jnp.float32).astype(jnp.bfloat16)
        running = running + rotated.astype(jnp.float32)
    consensus = (running / CKPTS).astype(jnp.bfloat16)
    results = []
    for member in range(CKPTS):
        cov = jnp.dot(aligned_list[member].T, consensus, preferred_element_type=jnp.float32)
        scale_now = 2.0 * jnp.sqrt(jnp.sum(cov * cov) / W + 1e-06)
        start_mat = (cov / scale_now).astype(jnp.bfloat16)
        first = 1.5 * start_mat.astype(jnp.float32) - 0.5 * apply_once(start_mat, start_mat)
        upper = 1.5 * first - 0.5 * apply_once(first, start_mat)
        middle = apply_once(upper, start_mat)
        cubic = 1.5 * middle - 0.5 * apply_once(middle, start_mat)
        results.append((math.sqrt(W) * (1.5 * first - 0.5 * cubic)).astype(jnp.bfloat16))
    return (consensus, jnp.stack(results, axis=0))
```

```python
import functools
import math

import jax
import jax.numpy as jnp
from jax import lax
from jax.experimental import pallas as pl
from jax.experimental.pallas import tpu as pltpu
from jax.sharding import PartitionSpec as P

MESH = pl.DeviceIdType.MESH
BF16, F32 = jnp.bfloat16, jnp.float32
W = 1792
H = W // 2
ROWS = 28
PAD = 32
T = 128
BLK = 112
N_SEM = 128


def dot(left, right):
    return jnp.dot(left, right, preferred_element_type=F32)


def dot_nt(left, right):
    return lax.dot_general(left, right, (((1,), (1,)), ((), ())), preferred_element_type=F32)


def m4(value):
    return lax.rem(value + 8, 4)


def kernel(
    feat, pair, rot, cons_out, next_out,
    rbuf, rsend, apad, at, racc, rotq, rotr, cons, crx,
    tx1, rx1, tx2, rx2, acc, tx3, rx3, tx4, rx4, txz, rxz, sbuf,
    ptx, prx, qtx, qrx, ofin, orx, ssem, rsem,
):
    ck = lax.axis_index("ckpt")
    tok = lax.axis_index("tok")
    core = lax.rem(tok, 2)
    x = lax.rem(lax.div(tok, 2), 4)
    zh = lax.rem(lax.div(tok, 8), 2)
    y = lax.div(tok, 16)
    a = x + core * (y - x)
    b = y + core * (x - y)

    def xy(i, j):
        return i + core * (j - i), j + core * (i - j)

    def chip(i, j, plane):
        px, py = xy(m4(i), m4(j))
        return (py * 2 + plane) * 4 + px

    def dev(i, j):
        return (ck, chip(i, j, zh) * 2 + core)

    right1, left1, right2, left2 = dev(a + 1, b), dev(a - 1, b), dev(a, b + 1), dev(a, b - 1)
    other = (ck, tok + 1 - 2 * core)
    far = (ck, ((y * 2 + 1 - zh) * 4 + x) * 2 + core)
    members = [m4(ck + d) for d in (1, 2, 3)]

    barrier = pltpu.get_barrier_semaphore()
    partners = [right1, left1, right2, left2, other, far] + [(m, tok) for m in members]
    for device in partners:
        pl.semaphore_signal(barrier, inc=1, device_id=device, device_id_type=MESH)
    pl.semaphore_wait(barrier, len(partners))

    sends = []

    def send(src, dst, device):
        slot = len(sends)
        assert slot < N_SEM
        copy = pltpu.make_async_remote_copy(
            src_ref=src,
            dst_ref=dst,
            send_sem=ssem.at[slot],
            recv_sem=rsem.at[slot],
            device_id=device,
            device_id_type=MESH,
        )
        copy.start()
        sends.append(copy)
        return copy

    def gather(part, meanwhile=None):
        def move(i, j, k, device):
            ref = part(i, j, k)
            return send(ref, ref, device)

        first_r, first_l = move(a, b, None, right1), move(a, b, None, left1)
        second = {}

        def spread(i):
            second[i] = (move(a + i, b, None, right2), move(a + i, b, None, left2))

        halves = {}

        def relay(i):
            second[i][0].wait_recv()
            low = move(a + i, b - 1, 0, right2)
            second[i][1].wait_recv()
            high = move(a + i, b + 1, 1, left2)
            halves[i] = (low, high)

        spread(0)
        if meanwhile is not None:
            meanwhile()
        first_r.wait_recv()
        half_r = move(a - 1, b, 0, right1)
        spread(-1)
        first_l.wait_recv()
        half_l = move(a + 1, b, 1, left1)
        spread(1)
        relay(0)
        half_r.wait_recv()
        half_l.wait_recv()
        spread(2)
        for i in (-1, 1, 2):
            relay(i)
        for i in (0, -1, 1, 2):
            halves[i][0].wait_recv()
            halves[i][1].wait_recv()

    def halfcols(value, index):
        return jnp.where(index == 0, value[:, :H], value[:, H:])

    own_rot = rot[0].astype(F32)
    zeros = jnp.zeros((PAD - ROWS, H), BF16)
    rbuf[tok, 0:ROWS, :] = halfcols(own_rot, core).astype(BF16)
    rbuf[tok, ROWS:PAD, :] = zeros
    rsend[0:ROWS, :] = halfcols(own_rot, 1 - core).astype(BF16)
    rsend[ROWS:PAD, :] = zeros
    swap = send(rsend, rbuf.at[tok], other)

    def rot_part(plane):
        def part(i, j, k):
            base = chip(i, j, plane) * 2
            return rbuf.at[pl.ds(base, 2)] if k is None else rbuf.at[base + k]

        return part

    def align():
        order = pair[0]
        hot_t = lax.broadcasted_iota(jnp.int32, (T, T), 0) == jnp.broadcast_to(order, (T, T))
        hot = jnp.transpose(jnp.where(hot_t, 1.0, 0.0)).astype(BF16)
        for n in range(7):
            cols = dot(hot, feat[0, :, 256 * n : 256 * n + 256])
            at[core, 16 * n : 16 * n + 16] = jnp.transpose(cols).astype(BF16).reshape(16, 16, T)
        for g in range(8):
            start = (224 * g) // 128 * 128
            width = min(384, W - start)
            src = lax.broadcasted_iota(jnp.int32, (width, 256), 0)
            dst = lax.broadcasted_iota(jnp.int32, (width, 256), 1)
            row = dst & 31
            want = (224 * g - start) + (dst >> 5) * ROWS + row
            place = jnp.where((src == want) & (row < ROWS), 1.0, 0.0).astype(BF16)
            window = dot(hot, feat[0, :, start : start + width]).astype(BF16)
            apad[core, g] = dot(window, place).astype(BF16)

    swap.wait_recv()
    own_chunk = rot_part(zh)(a, b, None)
    far_chunk = send(own_chunk, own_chunk, far)
    gather(rot_part(zh), align)
    aligned = [send(apad.at[core], apad.at[core], other), send(at.at[core], at.at[core], other)]
    far_chunk.wait_recv()
    gather(rot_part(1 - zh))
    for copy in aligned:
        copy.wait_recv()

    racc[...] = jnp.zeros_like(racc)

    def rotate(g, carry):
        left = jnp.concatenate([apad[0, g], apad[1, g]], axis=0)
        racc[...] += dot(left, rbuf[pl.ds(8 * g, 8)].reshape(8 * PAD, H))
        return carry

    lax.fori_loop(0, 8, rotate, 0)
    rotq[...] = racc[...].astype(BF16).reshape(4, 64, H)

    quarters = [send(rotq.at[m], rotr.at[ck], (m, tok)) for m in members]
    total = rotq[ck].astype(F32)
    for d, copy in zip((3, 2, 1), quarters):
        copy.wait_recv()
        total += rotr[m4(ck + d)].astype(F32)
    cons[ck] = (total * 0.25).astype(BF16)
    quarters = [send(cons.at[ck], cons.at[ck], (m, tok)) for m in members]
    for copy in quarters:
        copy.wait_recv()
    back = send(cons.at[pl.ds(2 * (1 - core), 2)], crx, other)

    cvalue = cons[...].reshape(2 * T, H)

    def block(i, j):
        px, py = xy(m4(i), m4(j))
        return (py * 4 + px) * 7

    def local(i, j):
        n = block(i, j)
        left = jnp.concatenate(
            [at[0, pl.ds(n, 7)].reshape(BLK, T), at[1, pl.ds(n, 7)].reshape(BLK, T)], axis=1
        )
        return dot(left, cvalue)

    def tiles(value):
        return value.astype(BF16).reshape(-1, 16, H)

    def wide(value):
        return value.astype(F32).reshape(-1, H)

    order = (2, 1, -1, 0)
    step1 = []
    for n, j in enumerate(order):
        tx1[n] = tiles(local(a + 2, b + j))
        step1.append(
            (
                send(tx1.at[n, 0:4], rx1.at[n, 0:4], right1),
                send(tx1.at[n, 4:7], rx1.at[n, 4:7], left1),
            )
        )
    step2 = []
    for n, j in enumerate(order):
        acc[...] = local(a + 1, b + j)
        step1[n][0].wait_recv()
        acc[0:64] += wide(rx1[n, 0:4])
        tx2[0, n] = tiles(acc[...])
        to_right = send(tx2.at[0, n], rx2.at[0, n], right1)
        acc[...] = local(a - 1, b + j)
        step1[n][1].wait_recv()
        acc[64:112] += wide(rx1[n, 4:7])
        tx2[1, n] = tiles(acc[...])
        step2.append((to_right, send(tx2.at[1, n], rx2.at[1, n], left1)))

    def along(n):
        value = local(a, b + order[n])
        step2[n][0].wait_recv()
        step2[n][1].wait_recv()
        return value + wide(rx2[0, n]) + wide(rx2[1, n])

    tx3[...] = tiles(along(0))
    step3 = (send(tx3.at[0:4], rx3.at[0:4], right2), send(tx3.at[4:7], rx3.at[4:7], left2))
    acc[...] = along(1)
    step3[0].wait_recv()
    acc[0:64] += wide(rx3[0:4])
    tx4[0] = tiles(acc[...])
    to_right = send(tx4.at[0], rx4.at[0], right2)
    acc[...] = along(2)
    step3[1].wait_recv()
    acc[64:112] += wide(rx3[4:7])
    tx4[1] = tiles(acc[...])
    to_left = send(tx4.at[1], rx4.at[1], left2)
    acc[...] = along(3)
    to_right.wait_recv()
    to_left.wait_recv()
    acc[...] += wide(rx4[0]) + wide(rx4[1])
    txz[...] = tiles(acc[...])
    across = send(txz, rxz, far)
    back.wait_recv()

    @pl.when(core == 0)
    def _():
        cons_out[:, :H] = cons[0:2].reshape(T, H)
        cons_out[:, H:] = crx[...].reshape(T, H)

    @pl.when(core == 1)
    def _():
        cons_out[:, H:] = cons[2:4].reshape(T, H)
        cons_out[:, :H] = crx[...].reshape(T, H)

    across.wait_recv()
    own_block = block(a, b)
    sbuf[pl.ds(own_block, 7)] = tiles(acc[...] + wide(rxz[...]))

    def cov_part(i, j, k):
        n = block(i, j)
        if k is None:
            return sbuf.at[pl.ds(n, 7)]
        return sbuf.at[pl.ds(n, 4)] if k == 0 else sbuf.at[pl.ds(n + 4, 3)]

    gather(cov_part)

    def rows(n):
        return sbuf[16 * n : 16 * n + 16].reshape(256, H)

    square = jnp.zeros((1, H), F32)
    for n in range(7):
        value = rows(n).astype(F32)
        square += jnp.sum(value * value, axis=0, keepdims=True)
    qtx[...] = jnp.broadcast_to(jnp.sum(square, axis=1, keepdims=True), (8, 128))
    squares = send(qtx, qrx, other)

    px, py = x, y
    base = (py * 4 + zh * 2 + lax.div(px, 2)) * 7
    dst = lax.broadcasted_iota(jnp.int32, (2 * PAD, BLK), 0)
    src = lax.broadcasted_iota(jnp.int32, (2 * PAD, BLK), 1)
    row = dst & 31
    want = 56 * lax.rem(px, 2) + (dst >> 5) * ROWS + row
    pick = jnp.where((src == want) & (row < ROWS), 1.0, 0.0).astype(BF16)
    raw = dot(pick, sbuf[pl.ds(base, 7)].reshape(BLK, H))

    def apply(vector, n):
        low = vector.astype(BF16)
        for k in range(7):
            ptx[n, :, 256 * k : 256 * k + 256] = dot_nt(low, rows(k))
        copy = send(ptx.at[n], prx.at[n], other)
        copy.wait_recv()
        inner = (ptx[n] + prx[n]).astype(BF16)
        result = dot(inner[:, 0:256], rows(0))
        for k in range(1, 7):
            result += dot(inner[:, 256 * k : 256 * k + 256], rows(k))
        return result

    once = apply(raw, 0)
    squares.wait_recv()
    scale = 2.0 * jnp.sqrt((qtx[0:1, 0:1] + qrx[0:1, 0:1]) / W + 1e-06)
    inverse = 1.0 / scale
    square_inverse = inverse * inverse
    first = (1.5 * raw - 0.5 * (once * square_inverse)) * inverse
    upper = 1.5 * first - 0.5 * (apply(first, 1) * square_inverse)
    middle = apply(upper, 2) * square_inverse
    cubic = 1.5 * middle - 0.5 * (apply(middle, 3) * square_inverse)
    ofin[...] = (math.sqrt(W) * (1.5 * first - 0.5 * cubic)).astype(BF16).reshape(2, PAD, H)
    final = send(ofin.at[1 - core], orx, other)
    final.wait_recv()

    @pl.when(core == 0)
    def _():
        next_out[0, :, :H] = ofin[0, 0:ROWS]
        next_out[0, :, H:] = orx[0:ROWS]

    @pl.when(core == 1)
    def _():
        next_out[0, :, H:] = ofin[1, 0:ROWS]
        next_out[0, :, :H] = orx[0:ROWS]

    for copy in sends:
        copy.wait_send()


def shards(features, pairing, rotation):
    vmem = pl.BlockSpec(memory_space=pltpu.VMEM)
    return pl.pallas_call(
        kernel,
        out_shape=(
            jax.ShapeDtypeStruct((T, W), BF16),
            jax.ShapeDtypeStruct((1, ROWS, W), BF16),
        ),
        in_specs=[vmem] * 3,
        out_specs=(vmem, vmem),
        scratch_shapes=[
            pltpu.VMEM((64, PAD, H), BF16),
            pltpu.VMEM((PAD, H), BF16),
            pltpu.VMEM((2, 8, T, 256), BF16),
            pltpu.VMEM((2, 112, 16, T), BF16),
            pltpu.VMEM((2 * T, H), F32),
            pltpu.VMEM((4, 64, H), BF16),
            pltpu.VMEM((4, 64, H), BF16),
            pltpu.VMEM((4, 64, H), BF16),
            pltpu.VMEM((2, 64, H), BF16),
            pltpu.VMEM((4, 7, 16, H), BF16),
            pltpu.VMEM((4, 7, 16, H), BF16),
            pltpu.VMEM((2, 4, 7, 16, H), BF16),
            pltpu.VMEM((2, 4, 7, 16, H), BF16),
            pltpu.VMEM((BLK, H), F32),
            pltpu.VMEM((7, 16, H), BF16),
            pltpu.VMEM((7, 16, H), BF16),
            pltpu.VMEM((2, 7, 16, H), BF16),
            pltpu.VMEM((2, 7, 16, H), BF16),
            pltpu.VMEM((7, 16, H), BF16),
            pltpu.VMEM((7, 16, H), BF16),
            pltpu.VMEM((112, 16, H), BF16),
            pltpu.VMEM((4, 2 * PAD, W), F32),
            pltpu.VMEM((4, 2 * PAD, W), F32),
            pltpu.VMEM((8, 128), F32),
            pltpu.VMEM((8, 128), F32),
            pltpu.VMEM((2, PAD, H), BF16),
            pltpu.VMEM((PAD, H), BF16),
            pltpu.SemaphoreType.DMA((N_SEM,)),
            pltpu.SemaphoreType.DMA((N_SEM,)),
        ],
        compiler_params=pltpu.CompilerParams(
            collective_id=0, has_side_effects=True, vmem_limit_bytes=60 * 1024 * 1024
        ),
    )(features, pairing, rotation)


def solution(mesh):
    placed = (P("ckpt", "tok", None), P("ckpt", "tok", None), P("ckpt", "tok", None))
    return jax.shard_map(
        shards,
        mesh=mesh,
        in_specs=placed,
        out_specs=(P("tok", None), P("ckpt", "tok", None)),
        check_vma=False,
    )
```

```python
import heapq
import math

import jax
import jax.numpy as jnp
from jax import lax
from jax.experimental import pallas as pl
from jax.experimental.pallas import tpu as pltpu
from jax.sharding import PartitionSpec as P

MESH = pl.DeviceIdType.MESH
BF16, F32 = jnp.bfloat16, jnp.float32
W = 1792
H = W // 2
ROWS = 28
PAD = 32
T = 128
BLK = 112
WIDTHS = (256, 256, 256, 128)
STARTS = tuple(sum(WIDTHS[:p]) for p in range(len(WIDTHS)))
PARTS = range(len(WIDTHS))
N_SEND, N_RECV = 48, 220
NEAR1 = (0, 1, 2, 3)
GFAST = (0,)
FAST = (3,)

RATE, CHIP_RATE = 90e3, 600e3
HOP, CHIP_HOP, FURTHER = 2.4, 1.6, 0.7
BACKLOG = 0.3
GROUPS = {1: 2, 3: 2, 5: 2, 6: 1}


def scratch():
    out = []
    for p, w in enumerate(WIDTHS):
        for name, shape, dtype in (
            ("rbuf", (64, PAD, w), BF16),
            ("rsend", (PAD, w), BF16),
            ("rotq", (4, 64, w), BF16),
            ("rotr", (4, 64, w), BF16),
            ("cons", (4, 64, w), BF16),
            ("crx", (2, 64, w), BF16),
            ("tx1", (4, 7, 16, w), BF16),
            ("rx1", (4, 7, 16, w), BF16),
            ("tx2", (2, 4, 7, 16, w), BF16),
            ("rx2", (2, 4, 7, 16, w), BF16),
            ("acc", (3, 4, BLK, w), F32),
            ("tx3", (7, 16, w), BF16),
            ("rx3", (7, 16, w), BF16),
            ("tx4", (2, 7, 16, w), BF16),
            ("rx4", (2, 7, 16, w), BF16),
            ("txz", (7, 16, w), BF16),
            ("rxz", (7, 16, w), BF16),
            ("sbuf", (112, 16, w), BF16),
            ("ofin", (2, PAD, w), BF16),
            ("orx", (PAD, w), BF16),
            ("racc", (2 * T, w), F32),
        ):
            out.append(((name, p), pltpu.VMEM(shape, dtype)))
    out += [
        (("aown", None), pltpu.VMEM((T, W), BF16)),
        (("apad", None), pltpu.VMEM((2, 8, T, 256), BF16)),
        (("at", None), pltpu.VMEM((2, 112, 16, T), BF16)),
        (("ptx", None), pltpu.VMEM((4, 7, 2 * PAD, 256), F32)),
        (("prx", None), pltpu.VMEM((4, 7, 2 * PAD, 256), F32)),
        (("qtx", None), pltpu.VMEM((8, 128), F32)),
        (("qrx", None), pltpu.VMEM((8, 128), F32)),
        (("ssem", None), pltpu.SemaphoreType.DMA((N_SEND,))),
        (("rsem", None), pltpu.SemaphoreType.DMA((N_RECV,))),
    ]
    return out


def dot(left, right):
    return jnp.dot(left, right, preferred_element_type=F32)


def dot_nt(left, right):
    return lax.dot_general(left, right, (((1,), (1,)), ((), ())), preferred_element_type=F32)


def m4(value):
    return lax.rem(value + 8, 4)


class Timeline:
    def __init__(self, ssem, rsem):
        self.ssem, self.rsem = ssem, rsem
        self.now, self.free, self.queue, self.idle, self.sends = 0.0, {}, [], [], []
        self.pushed = self.slots = 0

    def cost(self, us):
        self.now += us

    def slot(self):
        self.slots += 1
        assert self.slots <= N_RECV
        return self.slots - 1

    def send(self, src, dst, device, lane, slot=None):
        turn = len(self.sends)
        if turn >= N_SEND:
            self.sends[turn - N_SEND].wait_send()
        copy = pltpu.make_async_remote_copy(
            src_ref=src,
            dst_ref=dst,
            send_sem=self.ssem.at[turn % N_SEND],
            recv_sem=self.rsem.at[self.slot() if slot is None else slot],
            device_id=device,
            device_id_type=MESH,
        )
        copy.start()
        self.sends.append(copy)
        size = math.prod(src.shape) * jnp.dtype(src.dtype).itemsize
        names, rate, latency = {
            "R": ("R", RATE, HOP),
            "L": ("L", RATE, HOP),
            "RL": ("RL", RATE, HOP + FURTHER),
            "core": ("C", CHIP_RATE, CHIP_HOP),
            "z": ("Z", RATE / 2, HOP + FURTHER),
            "far": ("Z", RATE / 4, HOP + 3 * FURTHER),
        }[lane]
        self.now += 0.02
        for name in names:
            self.free[name] = max(self.now, self.free.get(name, 0.0)) + size / rate
        return copy.wait_recv, max(self.free[name] for name in names) + latency

    def together(self, slot, ref, sent):
        return pltpu.make_async_copy(ref, ref, self.rsem.at[slot]).wait, max(arrival for _, arrival in sent)

    def finish(self):
        for copy in self.sends[-N_SEND:]:
            copy.wait_send()

    def after(self, sent, action):
        wait, arrival = sent
        self.pushed += 1
        heapq.heappush(self.queue, (arrival, self.pushed, wait, action))

    def later(self, rank, action):
        self.pushed += 1
        heapq.heappush(self.idle, (rank, self.pushed, action))

    def run(self):
        while self.queue or self.idle:
            if self.idle:
                quiet = max(self.free.get("R", 0.0), self.free.get("L", 0.0)) - BACKLOG
                if not self.queue or quiet <= max(self.now, self.queue[0][0]):
                    self.now = max(self.now, quiet)
                    heapq.heappop(self.idle)[2]()
                    continue
            arrival, _, wait, action = heapq.heappop(self.queue)
            self.now = max(self.now, arrival)
            wait()
            action()


def when_all(count, action):
    left = [count]

    def one():
        left[0] -= 1
        if not left[0]:
            action()

    return one


def nothing():
    pass


def kernel(feat, pair, rot, cons_out, next_out, *refs):
    buf = {name: ref for (name, _), ref in zip(scratch(), refs)}
    aown, apad, at, ptx, prx, qtx, qrx, ssem, rsem = [
        buf[name, None] for name in ("aown", "apad", "at", "ptx", "prx", "qtx", "qrx", "ssem", "rsem")
    ]
    ck = lax.axis_index("ckpt")
    tok = lax.axis_index("tok")
    core = lax.rem(tok, 2)
    x = lax.rem(lax.div(tok, 2), 4)
    zh = lax.rem(lax.div(tok, 8), 2)
    y = lax.div(tok, 16)
    a = x + core * (y - x)
    b = y + core * (x - y)

    def xy(i, j):
        i, j = m4(i), m4(j)
        return i + core * (j - i), j + core * (i - j)

    def chip(i, j, plane):
        px, py = xy(i, j)
        return (py * 2 + plane) * 4 + px

    def dev(i, j):
        return (ck, chip(i, j, zh) * 2 + core)

    right1, left1, right2, left2 = dev(a + 1, b), dev(a - 1, b), dev(a, b + 1), dev(a, b - 1)
    across1, across2 = dev(a + 2, b), dev(a, b + 2)
    other = (ck, tok + 1 - 2 * core)
    far, far_other = [(ck, ((y * 2 + 1 - zh) * 4 + x) * 2 + c) for c in (core, 1 - core)]
    members = [m4(ck + d) for d in (1, 2, 3)]

    barrier = pltpu.get_barrier_semaphore()
    partners = [right1, left1, across1, right2, left2, across2, other, far, far_other] + [(m, tok) for m in members]
    for device in partners:
        pl.semaphore_signal(barrier, inc=1, device_id=device, device_id_type=MESH)
    pl.semaphore_wait(barrier, len(partners))

    line = Timeline(ssem, rsem)
    send, after = line.send, line.after

    def gather(part, done, direct1, direct2):
        late, lates = line.slot(), []

        def move(i, j, k, device, lane, slot=None):
            ref = part(i, j, k)
            return send(ref, ref, device, lane, slot)

        def finish():
            after(line.together(late, part(None, None, 12 if direct2 else 4), lates), done)

        relayed = when_all(8, finish)

        def spread(i):
            if direct2:
                lates.append(move(a + i, b, None, right2, "R", late))
                lates.append(move(a + i, b, None, left2, "L", late))
                lates.append(move(a + i, b, None, across2, "RL", late))
                if len(lates) == 12:
                    finish()
                return

            def half():
                lates.append(move(a + i, b - 1, 0, right2, "R", late))
                relayed()

            def half_back():
                lates.append(move(a + i, b + 1, 1, left2, "L", late))
                relayed()

            after(move(a + i, b, None, right2, "R"), half)
            after(move(a + i, b, None, left2, "L"), half_back)

        def from_across():
            spread(2)

        halves, pair = [], None if direct1 else line.slot()
        both = when_all(2, lambda: after(line.together(pair, part(None, None, 1), halves), from_across))

        def from_left():
            if not direct1:
                halves.append(move(a - 1, b, 0, right1, "R", pair))
                both()
            spread(-1)

        def from_right():
            if not direct1:
                halves.append(move(a + 1, b, 1, left1, "L", pair))
                both()
            spread(1)

        after(move(a, b, None, right1, "R"), from_left)
        after(move(a, b, None, left1, "L"), from_right)
        if direct1:
            after(move(a, b, None, across1, "RL"), from_across)
        spread(0)

    swaps, fars = [], []
    for p, w in enumerate(WIDTHS):
        rbuf, rsend = buf["rbuf", p], buf["rsend", p]
        low = rot[0, :, STARTS[p] : STARTS[p] + w].astype(F32)
        high = rot[0, :, H + STARTS[p] : H + STARTS[p] + w].astype(F32)
        zeros = jnp.zeros((PAD - ROWS, w), BF16)
        rsend[0:ROWS, :] = jnp.where(core == 0, high, low).astype(BF16)
        rsend[ROWS:PAD, :] = zeros
        swaps.append(send(rsend, rbuf.at[tok], other, "core"))
        rbuf[tok, 0:ROWS, :] = jnp.where(core == 0, low, high).astype(BF16)
        rbuf[tok, ROWS:PAD, :] = zeros
        slot = line.slot()
        sent = [
            send(rsend, rbuf.at[tok], far_other, "far", slot),
            send(rbuf.at[tok], rbuf.at[tok], far, "far", slot),
        ]
        fars.append(line.together(slot, rbuf.at[pl.ds(0, 2)], sent))

    def begin(p):
        rbuf = buf["rbuf", p]

        def part(plane):
            def of(i, j, k):
                if i is None:
                    return rbuf.at[pl.ds(0, 2 * k)]
                base = chip(i, j, plane) * 2
                return rbuf.at[pl.ds(base, 2)] if k is None else rbuf.at[base + k]

            return of

        done = when_all(2 if p else 4, lambda: rotate(p))

        def near():
            gather(part(zh), done, p in NEAR1, p in GFAST)
            if p == 0:
                align(done)

        def distant():
            gather(part(1 - zh), done, p in NEAR1, p in GFAST)
            if p + 1 in PARTS:
                begin(p + 1)

        after(swaps[p], lambda: line.later(2 * p, near))
        after(fars[p], lambda: line.later(2 * p + 1, distant))

    def align(done):
        order = pair[0]
        hot_t = lax.broadcasted_iota(jnp.int32, (T, T), 0) == jnp.broadcast_to(order, (T, T))
        hot = jnp.transpose(jnp.where(hot_t, 1.0, 0.0)).astype(BF16)
        for n in range(7):
            aown[:, 256 * n : 256 * n + 256] = dot(hot, feat[0, :, 256 * n : 256 * n + 256]).astype(BF16)
        for g in range(8):
            start = (224 * g) // 128 * 128
            width = min(384, W - start)
            src = lax.broadcasted_iota(jnp.int32, (width, 256), 0)
            dst = lax.broadcasted_iota(jnp.int32, (width, 256), 1)
            row = dst & 31
            want = (224 * g - start) + (dst >> 5) * ROWS + row
            place = jnp.where((src == want) & (row < ROWS), 1.0, 0.0).astype(BF16)
            apad[core, g] = dot(aown[:, start : start + width], place).astype(BF16)
        dst = lax.broadcasted_iota(jnp.int32, (448, 512), 0)
        src = lax.broadcasted_iota(jnp.int32, (448, 512), 1)
        px = sum((dst >= BLK * n).astype(jnp.int32) for n in (1, 2, 3))
        dst = dst - BLK * px
        plane = (dst >= 56).astype(jnp.int32)
        want = 224 * plane + 56 * px + dst - 56 * plane
        places = [jnp.where(src == want + offset, 1.0, 0.0).astype(BF16) for offset in (0, 64)]
        for n in range(4):
            start = 448 * n // 128 * 128
            window = dot_nt(places[n % 2], aown[:, start : start + 512])
            at[core, 28 * n : 28 * n + 28] = window.astype(BF16).reshape(28, 16, T)
        after(send(apad.at[core], apad.at[core], other, "core"), done)
        after(send(at.at[core], at.at[core], other, "core"), done)
        line.cost(3.0)

    def rotate(p):
        w, racc, rbuf, rotq, rotr = WIDTHS[p], buf["racc", p], buf["rbuf", p], buf["rotq", p], buf["rotr", p]
        racc[...] = jnp.zeros_like(racc)

        def step(g, carry):
            left = jnp.concatenate([apad[0, g], apad[1, g]], axis=0)
            racc[...] += dot(left, rbuf[pl.ds(8 * g, 8)].reshape(8 * PAD, w))
            return carry

        lax.fori_loop(0, 8, step, 0)
        rotq[...] = racc[...].astype(BF16).reshape(4, 64, w)
        line.cost(w / 300)
        slot = line.slot()
        sent = [send(rotq.at[m], rotr.at[ck], (m, tok), "z", slot) for m in members]
        after(line.together(slot, rotr.at[pl.ds(0, 3)], sent), lambda: mean(p))

    def mean(p):
        rotq, rotr, cons, crx = buf["rotq", p], buf["rotr", p], buf["cons", p], buf["crx", p]
        total = rotq[ck].astype(F32)
        for m in members:
            total += rotr[m].astype(F32)
        cons[ck] = (total * 0.25).astype(BF16)
        line.cost(0.2)

        def whole():
            after(send(cons.at[pl.ds(2 * (1 - core), 2)], crx, other, "core"), lambda: store(p))
            line.later(10 + p, lambda: reduce_plane(p))

        slot = line.slot()
        sent = [send(cons.at[ck], cons.at[ck], (m, tok), "z", slot) for m in members]
        after(line.together(slot, cons.at[pl.ds(0, 3)], sent), whole)

    def store(p):
        w, cons, crx = WIDTHS[p], buf["cons", p], buf["crx", p]
        low, high = slice(STARTS[p], STARTS[p] + w), slice(H + STARTS[p], H + STARTS[p] + w)

        @pl.when(core == 0)
        def _():
            cons_out[:, low] = cons[0:2].reshape(T, w)
            cons_out[:, high] = crx[...].reshape(T, w)

        @pl.when(core == 1)
        def _():
            cons_out[:, high] = cons[2:4].reshape(T, w)
            cons_out[:, low] = crx[...].reshape(T, w)

        line.cost(0.1)

    def block(i, j):
        px, py = xy(i, j)
        return (py * 4 + px) * 7

    order = (2, 1, -1, 0)

    def reduce_plane(p):
        w = WIDTHS[p]
        tx1, rx1, tx2, rx2, acc = [buf[name, p] for name in ("tx1", "rx1", "tx2", "rx2", "acc")]
        tx3, rx3, tx4, rx4, txz, rxz = [buf[name, p] for name in ("tx3", "rx3", "tx4", "rx4", "txz", "rxz")]
        cvalue = buf["cons", p][...].reshape(2 * T, w)

        def local(i):
            sides = []
            for k in range(2):
                sides.append(
                    jnp.concatenate([at[k, pl.ds(block(i, b + j), 7)].reshape(BLK, T) for j in order], axis=0)
                )
            line.cost(w / 500)
            return dot(jnp.concatenate(sides, axis=1), cvalue).reshape(4, BLK, w)

        def tiles(value):
            return value.astype(BF16).reshape(-1, 16, w)

        def wide(value):
            return value.astype(F32).reshape(-1, w)

        acc[0] = local(a + 2)
        tx1[...] = acc[0].astype(BF16).reshape(4, 7, 16, w)

        def final():
            txz[...] = tiles(acc[2, 3])
            line.cost(0.2)
            after(send(txz, rxz, far, "far"), lambda: spread_cov(p))

        direct2 = p in NEAR1
        slot, sent = line.slot(), []

        def last():
            if len(sent) == (3 if direct2 else 2):
                after(line.together(slot, tx2.at[0, 0 : len(sent)], sent), total)

        def total():
            acc[2, 3] += wide(rx4[0]) + wide(rx4[1])
            if direct2:
                acc[2, 3] += wide(rx3[...])
            line.cost(0.2)
            finals()

        finals = when_all(2, final)
        back = [when_all(1 if direct2 else 2, lambda: go_right()), when_all(1 if direct2 else 2, lambda: go_left())]

        def go_right():
            if not direct2:
                acc[2, 1, 0:64] += wide(rx3[0:4])
            tx4[0] = tiles(acc[2, 1])
            line.cost(0.1)
            sent.append(send(tx4.at[0], rx4.at[0], right2, "R", slot))
            last()

        def go_left():
            if not direct2:
                acc[2, 2, 64:112] += wide(rx3[4:7])
            tx4[1] = tiles(acc[2, 2])
            line.cost(0.1)
            sent.append(send(tx4.at[1], rx4.at[1], left2, "L", slot))
            last()

        def go_across():
            tx3[...] = tiles(acc[2, 0])
            if direct2:
                sent.append(send(tx3, rx3, across2, "RL", slot))
                last()
                return
            after(send(tx3.at[0:4], rx3.at[0:4], right2, "R"), back[0])
            after(send(tx3.at[4:7], rx3.at[4:7], left2, "L"), back[1])

        then = (go_across, back[0], back[1], finals)

        if p in FAST:
            slots = [line.slot() for _ in range(4)]
            sents = [[send(tx1.at[n], rx1.at[n], across1, "RL", slots[n])] for n in range(4)]
            for side, (device, lane) in enumerate(((right1, "R"), (left1, "L"))):
                acc[side] = local(a + 1 - 2 * side)
                tx2[side] = acc[side].astype(BF16).reshape(4, 7, 16, w)
                for n in range(4):
                    sents[n].append(send(tx2.at[side, n], rx2.at[side, n], device, lane, slots[n]))
            acc[2] = local(a)

            def column(n):
                def add():
                    acc[2, n] += wide(rx1[n]) + wide(rx2[0, n]) + wide(rx2[1, n])
                    line.cost(0.2)
                    then[n]()

                after(line.together(slots[n], tx1.at[0:3], sents[n]), add)

            for n in range(4):
                column(n)
            return

        firsts = [
            (
                send(tx1.at[n, 0:4], rx1.at[n, 0:4], right1, "R"),
                send(tx1.at[n, 4:7], rx1.at[n, 4:7], left1, "L"),
            )
            for n in range(4)
        ]
        acc[0] = local(a + 1)
        acc[1] = local(a - 1)
        acc[2] = local(a)

        def column(n):
            slot, sent = line.slot(), []

            def add():
                acc[2, n] += wide(rx2[0, n]) + wide(rx2[1, n])
                line.cost(0.15)
                then[n]()

            def sent_both():
                if len(sent) == 2:
                    after(line.together(slot, rx2.at[:, n], sent), add)

            def to_right():
                acc[0, n, 0:64] += wide(rx1[n, 0:4])
                tx2[0, n] = tiles(acc[0, n])
                line.cost(0.1)
                sent.append(send(tx2.at[0, n], rx2.at[0, n], right1, "R", slot))
                sent_both()

            def to_left():
                acc[1, n, 64:112] += wide(rx1[n, 4:7])
                tx2[1, n] = tiles(acc[1, n])
                line.cost(0.1)
                sent.append(send(tx2.at[1, n], rx2.at[1, n], left1, "L", slot))
                sent_both()

            after(firsts[n][0], to_right)
            after(firsts[n][1], to_left)

        for n in range(4):
            column(n)

    def spread_cov(p):
        w, acc, rxz, sbuf = WIDTHS[p], buf["acc", p], buf["rxz", p], buf["sbuf", p]
        total = acc[2, 3] + rxz[...].astype(F32).reshape(BLK, w)
        sbuf[pl.ds(block(a, b), 7)] = total.astype(BF16).reshape(7, 16, w)
        line.cost(0.2)

        def part(i, j, k):
            if i is None:
                return sbuf.at[pl.ds(0, 7 * k)]
            n = block(i, j)
            if k is None:
                return sbuf.at[pl.ds(n, 7)]
            return sbuf.at[pl.ds(n, 4)] if k == 0 else sbuf.at[pl.ds(n + 4, 3)]

        gather(part, lambda: begin_steps(p), p in NEAR1, p in FAST)

    dst = lax.broadcasted_iota(jnp.int32, (2 * PAD, BLK), 0)
    src = lax.broadcasted_iota(jnp.int32, (2 * PAD, BLK), 1)
    row = dst & 31
    pick = jnp.where((src == 56 * zh + (dst >> 5) * ROWS + row) & (row < ROWS), 1.0, 0.0).astype(BF16)
    raws, squares, seen = {}, [], []

    def rows(p, k):
        return buf["sbuf", p][16 * k : 16 * k + 16].reshape(256, WIDTHS[p])

    def begin_steps(p):
        raws[p] = dot(pick, buf["sbuf", p][pl.ds(block(a, b), 7)].reshape(BLK, WIDTHS[p]))
        square = jnp.zeros((1, WIDTHS[p]), F32)
        for k in range(7):
            value = rows(p, k)
            partial = dot_nt(raws[p].astype(BF16), value)
            ptx[0, k] = ptx[0, k] + partial if seen else partial
            if len(seen) + 1 == len(WIDTHS):
                exchange(0, k)
            value = value.astype(F32)
            square += jnp.sum(value * value, axis=0, keepdims=True)
        squares.append(jnp.sum(square, axis=1, keepdims=True))
        seen.append(p)
        line.cost(0.8)

    copies = [{} for _ in range(4)]

    def exchange(n, k):
        if k in GROUPS:
            group = pl.ds(k - GROUPS[k] + 1, GROUPS[k])
            copies[n][k - GROUPS[k] + 1] = send(ptx.at[n, group], prx.at[n, group], other, "core")

    begin(0)
    line.run()

    qtx[...] = jnp.broadcast_to(sum(squares), (8, 128))
    squared = send(qtx, qrx, other, "core")

    def span(k, count):
        return jnp.concatenate(
            [buf["sbuf", p][16 * k : 16 * (k + count)].reshape(256 * count, w) for p, w in enumerate(WIDTHS)], axis=1
        )

    def second_half(n):
        result = jnp.zeros((2 * PAD, H), F32)
        for last, count in GROUPS.items():
            k = last - count + 1
            copies[n][k][0]()
            inner = [(ptx[n, i] + prx[n, i]).astype(BF16) for i in range(k, last + 1)]
            result += dot(jnp.concatenate(inner, axis=1), span(k, count))
        return result

    def apply(vector, n):
        low = vector.astype(BF16)
        for k in range(7):
            ptx[n, k] = dot_nt(low, span(k, 1))
            exchange(n, k)
        return second_half(n)

    raw = jnp.concatenate([raws[p] for p in PARTS], axis=1)
    once = second_half(0)
    squared[0]()
    scale = 2.0 * jnp.sqrt((qtx[0:1, 0:1] + qrx[0:1, 0:1]) / W + 1e-06)
    inverse = 1.0 / scale
    square_inverse = inverse * inverse
    first = (1.5 * raw - 0.5 * (once * square_inverse)) * inverse
    upper = 1.5 * first - 0.5 * (apply(first, 1) * square_inverse)
    middle = apply(upper, 2) * square_inverse
    cubic = 1.5 * middle - 0.5 * (apply(middle, 3) * square_inverse)
    result = (math.sqrt(W) * (1.5 * first - 0.5 * cubic)).astype(BF16)
    finals = []
    for p, w in enumerate(WIDTHS):
        buf["ofin", p][...] = result[:, STARTS[p] : STARTS[p] + w].reshape(2, PAD, w)
        finals.append(send(buf["ofin", p].at[1 - core], buf["orx", p], other, "core"))
    for p, w in enumerate(WIDTHS):
        ofin, orx = buf["ofin", p], buf["orx", p]
        low, high = slice(STARTS[p], STARTS[p] + w), slice(H + STARTS[p], H + STARTS[p] + w)
        finals[p][0]()

        @pl.when(core == 0)
        def _():
            next_out[0, :, low] = ofin[0, 0:ROWS]
            next_out[0, :, high] = orx[0:ROWS]

        @pl.when(core == 1)
        def _():
            next_out[0, :, high] = ofin[1, 0:ROWS]
            next_out[0, :, low] = orx[0:ROWS]

    line.finish()


def shards(features, pairing, rotation):
    vmem = pl.BlockSpec(memory_space=pltpu.VMEM)
    return pl.pallas_call(
        kernel,
        out_shape=(
            jax.ShapeDtypeStruct((T, W), BF16),
            jax.ShapeDtypeStruct((1, ROWS, W), BF16),
        ),
        in_specs=[vmem] * 3,
        out_specs=(vmem, vmem),
        scratch_shapes=[spec for _, spec in scratch()],
        compiler_params=pltpu.CompilerParams(
            collective_id=0, has_side_effects=True, vmem_limit_bytes=60 * 1024 * 1024
        ),
    )(features, pairing, rotation)


def solution(mesh):
    placed = (P("ckpt", "tok", None), P("ckpt", "tok", None), P("ckpt", "tok", None))
    return jax.shard_map(
        shards,
        mesh=mesh,
        in_specs=placed,
        out_specs=(P("tok", None), P("ckpt", "tok", None)),
        check_vma=False,
    )
```

```python
import heapq
import math

import jax
import jax.numpy as jnp
from jax import lax
from jax.experimental import pallas as pl
from jax.experimental.pallas import tpu as pltpu
from jax.sharding import PartitionSpec as P

MESH = pl.DeviceIdType.MESH
BF16, F32 = jnp.bfloat16, jnp.float32
W = 1792
H = W // 2
ROWS = 28
PAD = 32
T = 128
BLK = 112
WIDTHS = (256, 256, 256, 128)
STARTS = tuple(sum(WIDTHS[:p]) for p in range(len(WIDTHS)))
PARTS = range(len(WIDTHS))
N_SEND, N_RECV = 32, 215
NEAR1 = (0, 1, 2, 3)
GFAST = (0,)
FAST = (3,)

RATE, CHIP_RATE = 84e3, 600e3
Z_RATE, FAR_RATE = 39e3, 21e3
HOP, CHIP_HOP, FURTHER = 2.9, 1.6, 0.8
BACKLOG = 0.3
GROUPS = {1: 2, 3: 2, 5: 2, 6: 1}


def scratch():
    out = []
    for p, w in enumerate(WIDTHS):
        for name, shape, dtype in (
            ("rbuf", (32, 2 * ROWS, w), BF16),
            ("rpart", (2, PAD, w), BF16),
            ("fpart", (2, PAD, w), BF16),
            ("rsend", (PAD, w), BF16),
            ("rotq", (4, 64, w), BF16),
            ("rotr", (4, 64, w), BF16),
            ("cons", (4, 64, w), BF16),
            ("crx", (2, 64, w), BF16),
            ("tx1", (4, 7, 16, w), BF16),
            ("rx1", (4, 7, 16, w), BF16),
            ("tx2", (2, 4, 7, 16, w), BF16),
            ("rx2", (2, 4, 7, 16, w), BF16),
            ("acc", (3, 4, BLK, w), F32),
            ("tx3", (7, 16, w), BF16),
            ("rx3", (7, 16, w), BF16),
            ("tx4", (2, 7, 16, w), BF16),
            ("rx4", (2, 7, 16, w), BF16),
            ("txz", (7, 16, w), BF16),
            ("rxz", (7, 16, w), BF16),
            ("sbuf", (112, 16, w), BF16),
            ("ofin", (2, PAD, w), BF16),
            ("orx", (PAD, w), BF16),
            ("racc", (2 * T, w), F32),
        ):
            out.append(((name, p), pltpu.VMEM(shape, dtype)))
    out += [
        (("aown", None), pltpu.VMEM((T, W), BF16)),
        (("apad", None), pltpu.VMEM((2, 8, T, 256), BF16)),
        (("at", None), pltpu.VMEM((2, 112, 16, T), BF16)),
        (("ptx", None), pltpu.VMEM((4, 7, 2 * PAD, 256), F32)),
        (("prx", None), pltpu.VMEM((4, 7, 2 * PAD, 256), F32)),
        (("qtx", None), pltpu.VMEM((8, 128), F32)),
        (("qrx", None), pltpu.VMEM((8, 128), F32)),
        (("ssem", None), pltpu.SemaphoreType.DMA((N_SEND,))),
        (("rsem", None), pltpu.SemaphoreType.DMA((N_RECV,))),
    ]
    return out


def dot(left, right):
    return jnp.dot(left, right, preferred_element_type=F32)


def dot_nt(left, right):
    return lax.dot_general(left, right, (((1,), (1,)), ((), ())), preferred_element_type=F32)


def m4(value):
    return lax.rem(value + 8, 4)


class Timeline:
    def __init__(self, ssem, rsem):
        self.ssem, self.rsem = ssem, rsem
        self.now, self.free, self.queue, self.idle, self.sends = 0.0, {}, [], [], []
        self.pushed = self.slots = 0

    def cost(self, us):
        self.now += us

    def slot(self):
        self.slots += 1
        assert self.slots <= N_RECV
        return self.slots - 1

    def send(self, src, dst, device, lane, slot=None):
        turn = len(self.sends)
        if turn >= N_SEND:
            self.sends[turn - N_SEND].wait_send()
        copy = pltpu.make_async_remote_copy(
            src_ref=src,
            dst_ref=dst,
            send_sem=self.ssem.at[turn % N_SEND],
            recv_sem=self.rsem.at[self.slot() if slot is None else slot],
            device_id=device,
            device_id_type=MESH,
        )
        copy.start()
        self.sends.append(copy)
        size = math.prod(src.shape) * jnp.dtype(src.dtype).itemsize
        names, rate, latency = {
            "R": ("R", RATE, HOP),
            "L": ("L", RATE, HOP),
            "RL": ("RL", RATE, HOP + FURTHER),
            "core": ("C", CHIP_RATE, CHIP_HOP),
            "z": ("Z", Z_RATE, HOP + FURTHER),
            "far": ("Z", FAR_RATE, HOP + 3 * FURTHER),
        }[lane]
        self.now += 0.02
        for name in names:
            self.free[name] = max(self.now, self.free.get(name, 0.0)) + size / rate
        return copy.wait_recv, max(self.free[name] for name in names) + latency

    def together(self, slot, ref, sent):
        return pltpu.make_async_copy(ref, ref, self.rsem.at[slot]).wait, max(arrival for _, arrival in sent)

    def finish(self):
        for copy in self.sends[-N_SEND:]:
            copy.wait_send()

    def after(self, sent, action):
        wait, arrival = sent
        self.pushed += 1
        heapq.heappush(self.queue, (arrival, self.pushed, wait, action))

    def later(self, rank, action):
        self.pushed += 1
        heapq.heappush(self.idle, (rank, self.pushed, action))

    def run(self):
        while self.queue or self.idle:
            if self.idle:
                quiet = max(self.free.get("R", 0.0), self.free.get("L", 0.0)) - BACKLOG
                if not self.queue or quiet <= max(self.now, self.queue[0][0]):
                    self.now = max(self.now, quiet)
                    heapq.heappop(self.idle)[2]()
                    continue
            arrival, _, wait, action = heapq.heappop(self.queue)
            self.now = max(self.now, arrival)
            wait()
            action()


def when_all(count, action):
    left = [count]

    def one():
        left[0] -= 1
        if not left[0]:
            action()

    return one


def nothing():
    pass


def kernel(feat, pair, rot, cons_out, next_out, *refs):
    buf = {name: ref for (name, _), ref in zip(scratch(), refs)}
    aown, apad, at, ptx, prx, qtx, qrx, ssem, rsem = [
        buf[name, None] for name in ("aown", "apad", "at", "ptx", "prx", "qtx", "qrx", "ssem", "rsem")
    ]
    ck = lax.axis_index("ckpt")
    tok = lax.axis_index("tok")
    core = lax.rem(tok, 2)
    x = lax.rem(lax.div(tok, 2), 4)
    zh = lax.rem(lax.div(tok, 8), 2)
    y = lax.div(tok, 16)
    a = x + core * (y - x)
    b = y + core * (x - y)

    def xy(i, j):
        i, j = m4(i), m4(j)
        return i + core * (j - i), j + core * (i - j)

    def chip(i, j, plane):
        px, py = xy(i, j)
        return (py * 2 + plane) * 4 + px

    def dev(i, j):
        return (ck, chip(i, j, zh) * 2 + core)

    right1, left1, right2, left2 = dev(a + 1, b), dev(a - 1, b), dev(a, b + 1), dev(a, b - 1)
    across1, across2 = dev(a + 2, b), dev(a, b + 2)
    other = (ck, tok + 1 - 2 * core)
    far, far_other = [(ck, ((y * 2 + 1 - zh) * 4 + x) * 2 + c) for c in (core, 1 - core)]
    members = [m4(ck + d) for d in (1, 2, 3)]

    barrier = pltpu.get_barrier_semaphore()
    partners = [right1, left1, across1, right2, left2, across2, other, far, far_other] + [(m, tok) for m in members]
    for device in partners:
        pl.semaphore_signal(barrier, inc=1, device_id=device, device_id_type=MESH)
    pl.semaphore_wait(barrier, len(partners))

    line = Timeline(ssem, rsem)
    send, after = line.send, line.after

    def gather(part, done, direct1, direct2):
        late, lates = line.slot(), []

        def move(i, j, k, device, lane, slot=None):
            ref = part(i, j, k)
            return send(ref, ref, device, lane, slot)

        def finish():
            after(line.together(late, part(None, None, 12 if direct2 else 4), lates), done)

        relayed = when_all(8, finish)

        def spread(i):
            if direct2:
                lates.append(move(a + i, b, None, right2, "R", late))
                lates.append(move(a + i, b, None, left2, "L", late))
                lates.append(move(a + i, b, None, across2, "RL", late))
                if len(lates) == 12:
                    finish()
                return

            def half():
                lates.append(move(a + i, b - 1, 0, right2, "R", late))
                relayed()

            def half_back():
                lates.append(move(a + i, b + 1, 1, left2, "L", late))
                relayed()

            after(move(a + i, b, None, right2, "R"), half)
            after(move(a + i, b, None, left2, "L"), half_back)

        def from_across():
            spread(2)

        halves, pair = [], None if direct1 else line.slot()
        both = when_all(2, lambda: after(line.together(pair, part(None, None, 1), halves), from_across))

        def from_left():
            if not direct1:
                halves.append(move(a - 1, b, 0, right1, "R", pair))
                both()
            spread(-1)

        def from_right():
            if not direct1:
                halves.append(move(a + 1, b, 1, left1, "L", pair))
                both()
            spread(1)

        after(move(a, b, None, right1, "R"), from_left)
        after(move(a, b, None, left1, "L"), from_right)
        if direct1:
            after(move(a, b, None, across1, "RL"), from_across)
        spread(0)

    dst = lax.broadcasted_iota(jnp.int32, (2 * ROWS, 2 * PAD), 0)
    src = lax.broadcasted_iota(jnp.int32, (2 * ROWS, 2 * PAD), 1)
    second = (dst >= ROWS).astype(jnp.int32)
    want = dst - ROWS * second + PAD * (second + core - 2 * core * second)
    order_rows = jnp.where(src == want, 1.0, 0.0).astype(BF16)

    def compose(p, plane, pieces):
        value = dot(order_rows, pieces[...].reshape(2 * PAD, WIDTHS[p]))
        buf["rbuf", p][chip(a, b, plane)] = value.astype(BF16)

    swaps, fars = [], []
    for p, w in enumerate(WIDTHS):
        rpart, fpart, rsend = buf["rpart", p], buf["fpart", p], buf["rsend", p]
        low = rot[0, :, STARTS[p] : STARTS[p] + w].astype(F32)
        high = rot[0, :, H + STARTS[p] : H + STARTS[p] + w].astype(F32)
        zeros = jnp.zeros((PAD - ROWS, w), BF16)
        rsend[0:ROWS, :] = jnp.where(core == 0, high, low).astype(BF16)
        rsend[ROWS:PAD, :] = zeros
        swaps.append(send(rsend, rpart.at[1], other, "core"))
        rpart[0, 0:ROWS, :] = jnp.where(core == 0, low, high).astype(BF16)
        rpart[0, ROWS:PAD, :] = zeros
        slot = line.slot()
        sent = [
            send(rsend, fpart.at[1], far_other, "far", slot),
            send(rpart.at[0], fpart.at[0], far, "far", slot),
        ]
        fars.append(line.together(slot, fpart, sent))

    def begin(p):
        rbuf = buf["rbuf", p]

        def part(plane):
            def of(i, j, k):
                if i is None:
                    return rbuf.at[pl.ds(0, k)]
                n = chip(i, j, plane)
                if k is None:
                    return rbuf.at[n]
                return rbuf.at[n, pl.ds(0, PAD)] if k == 0 else rbuf.at[n, pl.ds(PAD, 2 * ROWS - PAD)]

            return of

        done = when_all(2 if p else 4, lambda: rotate(p))

        def near():
            compose(p, zh, buf["rpart", p])
            gather(part(zh), done, p in NEAR1, p in GFAST)
            if p == 0:
                align(done)

        def distant():
            compose(p, 1 - zh, buf["fpart", p])
            gather(part(1 - zh), done, p in NEAR1, p in GFAST)
            if p + 1 in PARTS:
                begin(p + 1)

        after(swaps[p], lambda: line.later(2 * p, near))
        after(fars[p], lambda: line.later(2 * p + 1, distant))

    def align(done):
        order = pair[0]
        hot_t = lax.broadcasted_iota(jnp.int32, (T, T), 0) == jnp.broadcast_to(order, (T, T))
        hot = jnp.transpose(jnp.where(hot_t, 1.0, 0.0)).astype(BF16)
        for n in range(7):
            aown[:, 256 * n : 256 * n + 256] = dot(hot, feat[0, :, 256 * n : 256 * n + 256]).astype(BF16)
        for g in range(8):
            start = (224 * g) // 128 * 128
            width = min(384, W - start)
            src = lax.broadcasted_iota(jnp.int32, (width, 256), 0)
            dst = lax.broadcasted_iota(jnp.int32, (width, 256), 1)
            place = jnp.where((src == dst + (224 * g - start)) & (dst < 224), 1.0, 0.0).astype(BF16)
            apad[core, g] = dot(aown[:, start : start + width], place).astype(BF16)
        dst = lax.broadcasted_iota(jnp.int32, (448, 512), 0)
        src = lax.broadcasted_iota(jnp.int32, (448, 512), 1)
        px = sum((dst >= BLK * n).astype(jnp.int32) for n in (1, 2, 3))
        dst = dst - BLK * px
        plane = (dst >= 56).astype(jnp.int32)
        want = 224 * plane + 56 * px + dst - 56 * plane
        places = [jnp.where(src == want + offset, 1.0, 0.0).astype(BF16) for offset in (0, 64)]
        for n in range(4):
            start = 448 * n // 128 * 128
            window = dot_nt(places[n % 2], aown[:, start : start + 512])
            at[core, 28 * n : 28 * n + 28] = window.astype(BF16).reshape(28, 16, T)
        after(send(apad.at[core], apad.at[core], other, "core"), done)
        after(send(at.at[core], at.at[core], other, "core"), done)
        line.cost(1.2)

    def rotate(p):
        w, racc, rbuf, rotq, rotr = WIDTHS[p], buf["racc", p], buf["rbuf", p], buf["rotq", p], buf["rotr", p]
        for half in range(2):
            groups = range(4 * half, 4 * half + 4)
            left = jnp.concatenate([apad[:, g].reshape(2 * T, 256) for g in groups], axis=1)
            fill = jnp.zeros((256 - 8 * ROWS, w), BF16)
            right = []
            for g in groups:
                right += [rbuf[4 * g : 4 * g + 4].astype(F32).reshape(8 * ROWS, w).astype(BF16), fill]
            product = dot(left, jnp.concatenate(right, axis=0))
            racc[...] = racc[...] + product if half else product
        rotq[...] = racc[...].astype(BF16).reshape(4, 64, w)
        line.cost(w / 600)
        slot = line.slot()
        sent = [send(rotq.at[m], rotr.at[ck], (m, tok), "z", slot) for m in members]
        after(line.together(slot, rotr.at[pl.ds(0, 3)], sent), lambda: mean(p))

    def mean(p):
        rotq, rotr, cons, crx = buf["rotq", p], buf["rotr", p], buf["cons", p], buf["crx", p]
        total = rotq[ck].astype(F32)
        for m in members:
            total += rotr[m].astype(F32)
        cons[ck] = (total * 0.25).astype(BF16)
        line.cost(0.05)

        def whole():
            after(send(cons.at[pl.ds(2 * (1 - core), 2)], crx, other, "core"), lambda: store(p))
            line.later(10 + p, lambda: reduce_plane(p))

        slot = line.slot()
        sent = [send(cons.at[ck], cons.at[ck], (m, tok), "z", slot) for m in members]
        after(line.together(slot, cons.at[pl.ds(0, 3)], sent), whole)

    def store(p):
        w, cons, crx = WIDTHS[p], buf["cons", p], buf["crx", p]
        low, high = slice(STARTS[p], STARTS[p] + w), slice(H + STARTS[p], H + STARTS[p] + w)

        @pl.when(core == 0)
        def _():
            cons_out[:, low] = cons[0:2].reshape(T, w)
            cons_out[:, high] = crx[...].reshape(T, w)

        @pl.when(core == 1)
        def _():
            cons_out[:, high] = cons[2:4].reshape(T, w)
            cons_out[:, low] = crx[...].reshape(T, w)

        line.cost(0.03)

    def block(i, j):
        px, py = xy(i, j)
        return (py * 4 + px) * 7

    order = (2, 1, -1, 0)

    def reduce_plane(p):
        w = WIDTHS[p]
        tx1, rx1, tx2, rx2, acc = [buf[name, p] for name in ("tx1", "rx1", "tx2", "rx2", "acc")]
        tx3, rx3, tx4, rx4, txz, rxz = [buf[name, p] for name in ("tx3", "rx3", "tx4", "rx4", "txz", "rxz")]
        cvalue = buf["cons", p][...].reshape(2 * T, w)

        def local(i):
            sides = []
            for k in range(2):
                sides.append(
                    jnp.concatenate([at[k, pl.ds(block(i, b + j), 7)].reshape(BLK, T) for j in order], axis=0)
                )
            line.cost(w / 1500)
            return dot(jnp.concatenate(sides, axis=1), cvalue).reshape(4, BLK, w)

        def tiles(value):
            return value.astype(BF16).reshape(-1, 16, w)

        def wide(value):
            return value.astype(F32).reshape(-1, w)

        acc[0] = local(a + 2)
        tx1[...] = acc[0].astype(BF16).reshape(4, 7, 16, w)

        def final():
            txz[...] = tiles(acc[2, 3])
            line.cost(0.05)
            after(send(txz, rxz, far, "far"), lambda: spread_cov(p))

        direct2 = p in NEAR1
        slot, sent = line.slot(), []

        def last():
            if len(sent) == (3 if direct2 else 2):
                after(line.together(slot, tx2.at[0, 0 : len(sent)], sent), total)

        def total():
            acc[2, 3] += wide(rx4[0]) + wide(rx4[1])
            if direct2:
                acc[2, 3] += wide(rx3[...])
            line.cost(0.05)
            finals()

        finals = when_all(2, final)
        back = [when_all(1 if direct2 else 2, lambda: go_right()), when_all(1 if direct2 else 2, lambda: go_left())]

        def go_right():
            if not direct2:
                acc[2, 1, 0:64] += wide(rx3[0:4])
            tx4[0] = tiles(acc[2, 1])
            line.cost(0.03)
            sent.append(send(tx4.at[0], rx4.at[0], right2, "R", slot))
            last()

        def go_left():
            if not direct2:
                acc[2, 2, 64:112] += wide(rx3[4:7])
            tx4[1] = tiles(acc[2, 2])
            line.cost(0.03)
            sent.append(send(tx4.at[1], rx4.at[1], left2, "L", slot))
            last()

        def go_across():
            tx3[...] = tiles(acc[2, 0])
            if direct2:
                sent.append(send(tx3, rx3, across2, "RL", slot))
                last()
                return
            after(send(tx3.at[0:4], rx3.at[0:4], right2, "R"), back[0])
            after(send(tx3.at[4:7], rx3.at[4:7], left2, "L"), back[1])

        then = (go_across, back[0], back[1], finals)

        if p in FAST:
            slots = [line.slot() for _ in range(4)]
            sents = [[send(tx1.at[n], rx1.at[n], across1, "RL", slots[n])] for n in range(4)]
            for side, (device, lane) in enumerate(((right1, "R"), (left1, "L"))):
                acc[side] = local(a + 1 - 2 * side)
                tx2[side] = acc[side].astype(BF16).reshape(4, 7, 16, w)
                for n in range(4):
                    sents[n].append(send(tx2.at[side, n], rx2.at[side, n], device, lane, slots[n]))
            acc[2] = local(a)

            def column(n):
                def add():
                    acc[2, n] += wide(rx1[n]) + wide(rx2[0, n]) + wide(rx2[1, n])
                    line.cost(0.05)
                    then[n]()

                after(line.together(slots[n], tx1.at[0:3], sents[n]), add)

            for n in range(4):
                column(n)
            return

        firsts = [
            (
                send(tx1.at[n, 0:4], rx1.at[n, 0:4], right1, "R"),
                send(tx1.at[n, 4:7], rx1.at[n, 4:7], left1, "L"),
            )
            for n in range(4)
        ]
        acc[0] = local(a + 1)
        acc[1] = local(a - 1)
        acc[2] = local(a)

        def column(n):
            slot, sent = line.slot(), []

            def add():
                acc[2, n] += wide(rx2[0, n]) + wide(rx2[1, n])
                line.cost(0.04)
                then[n]()

            def sent_both():
                if len(sent) == 2:
                    after(line.together(slot, rx2.at[:, n], sent), add)

            def to_right():
                acc[0, n, 0:64] += wide(rx1[n, 0:4])
                tx2[0, n] = tiles(acc[0, n])
                line.cost(0.03)
                sent.append(send(tx2.at[0, n], rx2.at[0, n], right1, "R", slot))
                sent_both()

            def to_left():
                acc[1, n, 64:112] += wide(rx1[n, 4:7])
                tx2[1, n] = tiles(acc[1, n])
                line.cost(0.03)
                sent.append(send(tx2.at[1, n], rx2.at[1, n], left1, "L", slot))
                sent_both()

            after(firsts[n][0], to_right)
            after(firsts[n][1], to_left)

        for n in range(4):
            column(n)

    def spread_cov(p):
        w, acc, rxz, sbuf = WIDTHS[p], buf["acc", p], buf["rxz", p], buf["sbuf", p]
        total = acc[2, 3] + rxz[...].astype(F32).reshape(BLK, w)
        sbuf[pl.ds(block(a, b), 7)] = total.astype(BF16).reshape(7, 16, w)
        line.cost(0.05)

        def part(i, j, k):
            if i is None:
                return sbuf.at[pl.ds(0, 7 * k)]
            n = block(i, j)
            if k is None:
                return sbuf.at[pl.ds(n, 7)]
            return sbuf.at[pl.ds(n, 4)] if k == 0 else sbuf.at[pl.ds(n + 4, 3)]

        gather(part, lambda: begin_steps(p), p in NEAR1, p in FAST)

    dst = lax.broadcasted_iota(jnp.int32, (2 * PAD, BLK), 0)
    src = lax.broadcasted_iota(jnp.int32, (2 * PAD, BLK), 1)
    row = dst & 31
    pick = jnp.where((src == 56 * zh + (dst >> 5) * ROWS + row) & (row < ROWS), 1.0, 0.0).astype(BF16)
    raws, squares, seen = {}, [], []

    def rows(p, k):
        return buf["sbuf", p][16 * k : 16 * k + 16].reshape(256, WIDTHS[p])

    def begin_steps(p):
        raws[p] = dot(pick, buf["sbuf", p][pl.ds(block(a, b), 7)].reshape(BLK, WIDTHS[p]))
        square = jnp.zeros((1, WIDTHS[p]), F32)
        for k in range(7):
            value = rows(p, k)
            partial = dot_nt(raws[p].astype(BF16), value)
            ptx[0, k] = ptx[0, k] + partial if seen else partial
            if len(seen) + 1 == len(WIDTHS):
                exchange(0, k)
            value = value.astype(F32)
            square += jnp.sum(value * value, axis=0, keepdims=True)
        squares.append(jnp.sum(square, axis=1, keepdims=True))
        seen.append(p)
        line.cost(0.4)

    copies = [{} for _ in range(4)]

    def exchange(n, k):
        if k in GROUPS:
            group = pl.ds(k - GROUPS[k] + 1, GROUPS[k])
            copies[n][k - GROUPS[k] + 1] = send(ptx.at[n, group], prx.at[n, group], other, "core")

    begin(0)
    line.run()

    qtx[...] = jnp.broadcast_to(sum(squares), (8, 128))
    squared = send(qtx, qrx, other, "core")

    def span(k, count):
        return jnp.concatenate(
            [buf["sbuf", p][16 * k : 16 * (k + count)].reshape(256 * count, w) for p, w in enumerate(WIDTHS)], axis=1
        )

    def second_half(n):
        result = jnp.zeros((2 * PAD, H), F32)
        for last, count in GROUPS.items():
            k = last - count + 1
            copies[n][k][0]()
            inner = [(ptx[n, i] + prx[n, i]).astype(BF16) for i in range(k, last + 1)]
            result += dot(jnp.concatenate(inner, axis=1), span(k, count))
        return result

    def apply(vector, n):
        low = vector.astype(BF16)
        for k in range(7):
            ptx[n, k] = dot_nt(low, span(k, 1))
            exchange(n, k)
        return second_half(n)

    raw = jnp.concatenate([raws[p] for p in PARTS], axis=1)
    once = second_half(0)
    squared[0]()
    scale = 2.0 * jnp.sqrt((qtx[0:1, 0:1] + qrx[0:1, 0:1]) / W + 1e-06)
    inverse = 1.0 / scale
    square_inverse = inverse * inverse
    first = (1.5 * raw - 0.5 * (once * square_inverse)) * inverse
    upper = 1.5 * first - 0.5 * (apply(first, 1) * square_inverse)
    middle = apply(upper, 2) * square_inverse
    cubic = 1.5 * middle - 0.5 * (apply(middle, 3) * square_inverse)
    result = (math.sqrt(W) * (1.5 * first - 0.5 * cubic)).astype(BF16)
    finals = []
    for p, w in enumerate(WIDTHS):
        buf["ofin", p][...] = result[:, STARTS[p] : STARTS[p] + w].reshape(2, PAD, w)
        finals.append(send(buf["ofin", p].at[1 - core], buf["orx", p], other, "core"))
    for p, w in enumerate(WIDTHS):
        ofin, orx = buf["ofin", p], buf["orx", p]
        low, high = slice(STARTS[p], STARTS[p] + w), slice(H + STARTS[p], H + STARTS[p] + w)
        finals[p][0]()

        @pl.when(core == 0)
        def _():
            next_out[0, :, low] = ofin[0, 0:ROWS]
            next_out[0, :, high] = orx[0:ROWS]

        @pl.when(core == 1)
        def _():
            next_out[0, :, high] = ofin[1, 0:ROWS]
            next_out[0, :, low] = orx[0:ROWS]

    line.finish()


def keep(cons, following, cons_out, next_out):
    cons_out[...] = cons[...]
    next_out[...] = following[...]


def shards(features, pairing, rotation):
    vmem = pl.BlockSpec(memory_space=pltpu.VMEM)
    outs = pl.pallas_call(
        kernel,
        out_shape=(
            jax.ShapeDtypeStruct((T, W), BF16),
            jax.ShapeDtypeStruct((1, ROWS, W), BF16),
        ),
        in_specs=[vmem] * 3,
        out_specs=(vmem, vmem),
        scratch_shapes=[spec for _, spec in scratch()],
        compiler_params=pltpu.CompilerParams(
            collective_id=0, has_side_effects=True, vmem_limit_bytes=60 * 1024 * 1024
        ),
    )(features, pairing, rotation)
    return pl.pallas_call(
        keep,
        out_shape=tuple(jax.ShapeDtypeStruct(out.shape, out.dtype) for out in outs),
        in_specs=[vmem] * 2,
        out_specs=(vmem, vmem),
    )(*outs)


def solution(mesh):
    placed = (P("ckpt", "tok", None), P("ckpt", "tok", None), P("ckpt", "tok", None))
    return jax.shard_map(
        shards,
        mesh=mesh,
        in_specs=placed,
        out_specs=(P("tok", None), P("ckpt", "tok", None)),
        check_vma=False,
    )
```
